32 devices in a mesh: rows: 8 (over z, y), cols: 4 (over x, core).
Axes of the slice: x: 2, y: 2, z: 4, core: 2. Of those that a mesh axis runs over, the one named last changes fastest.
Arguments:
- sketches: bfloat16 [2048, 16384], P('rows', 'cols'), may hold values from -6 to 6, as said below
- start_basis: bfloat16 [16384, 256], P('cols'), may hold values from -6 to 6
- shrink_index: int32 [1], replicated, may hold values from 64 to 191
Outputs:
- shrunk: float32 [256, 16384], P('rows', 'cols')
The draws below stay inside these ranges and needn't reach their ends.
Inputs may be any that keep to these rules, and one draw needn't show every extreme that they name: `sketches`: real entries.
All inputs are finite; a program needn't handle non-finite values.
Results may differ from the reference program's by a relative error of at most 0.0028.
Values may be sent and summed in bfloat16 or wider, within the bound.
A program may use at most 64 MiB of HBM per device.

```python
import math
import jax
import jax.numpy as jnp
from jax import lax

W = 16384
L = 256
ITERS = 3
STACK = 2048


def draw_sketches(key, part):
    left_key, right_key = jax.random.split(jax.random.fold_in(key, 11))
    floor_key = jax.random.fold_in(key, 17)
    column_key = jax.random.fold_in(key, 23)
    row_key = jax.random.fold_in(key, 29)
    floor_level = 0.15
    column_scales = jnp.exp(jax.random.uniform(column_key, (W,), jnp.float32, -1.0, 0.7))
    ranks = jnp.arange(L, dtype=jnp.float32)
    ratios = jnp.exp(math.log(200.0) * (1.0 - ranks / (L - 1)))
    spectrum = floor_level * jnp.sqrt(ratios / min(STACK, W))
    left_factor = jax.random.normal(left_key, (STACK, L), jnp.float32)
    right_factor = jax.random.normal(right_key, (L, W), jnp.float32)
    noise = jax.random.normal(floor_key, (STACK, W), jnp.float32)
    row_scales = jnp.exp(jax.random.uniform(row_key, (STACK,), jnp.float32, 0.0, 1.0986123))
    signal = jnp.dot(left_factor * spectrum[None, :], right_factor)
    values = (signal + floor_level * noise) * row_scales[:, None] * column_scales[None, :]
    return jnp.clip(values, -6.0, 6.0).astype(jnp.bfloat16)


def block_scale(rng, extent, pieces, low, top_value):
    gain = 1.0
    for axis_at, shards_of in pieces:
        draws = jax.random.uniform(jax.random.fold_in(jax.random.fold_in(rng, 6), axis_at), (shards_of,), jnp.float32, low / len(pieces), top_value / len(pieces))
        gain = gain * jnp.repeat(jnp.exp(draws), extent[axis_at] // shards_of).reshape((-1,) + (1,) * (len(extent) - 1 - axis_at))
    return gain


def normal_values(key, dims, deviation, most, cuts=(), kind=jnp.bfloat16):
    drawn = jax.random.normal(key, dims, jnp.float32) * deviation
    if len(cuts) > 0:
        drawn = block_scale(key, dims, cuts, -0.22, 0.18) * drawn
    return jnp.clip(drawn, min=-most, max=most).astype(kind)


def setup_inputs(seed: int = 0) -> dict:
    seeds = jax.random.split(jax.random.key(seed), 4)
    sketches = draw_sketches(jax.random.fold_in(seeds[3], 71), 0)
    start_basis = normal_values(seeds[1], (W, L), 1.0, 6.0, ((0, 4),))
    shrink_index = jax.random.randint(seeds[2], (1,), L // 4, 3 * L // 4).astype(jnp.int32)
    return {"sketches": sketches, "start_basis": start_basis, "shrink_index": shrink_index}


def orthonormal(images, gram_total):
    lower_factor = jnp.linalg.cholesky(gram_total)
    return jax.scipy.linalg.solve_triangular(lower_factor, images.T, lower=True).T

def reference(sketches, start_basis, shrink_index):
    basis_bf = start_basis
    basis = start_basis.astype(jnp.float32)
    for loop_index in range(ITERS):
        projected = jnp.dot(sketches.astype(jnp.float32), basis_bf.astype(jnp.float32), preferred_element_type=jnp.float32)
        projected_bf = projected.astype(jnp.bfloat16)
        images = jnp.dot(sketches.T.astype(jnp.float32), projected_bf.astype(jnp.float32), preferred_element_type=jnp.float32)
        gram_total = jnp.dot(images.T, images, precision=lax.Precision.HIGHEST)
        basis = orthonormal(images, gram_total)
        basis_bf = basis.astype(jnp.bfloat16)
    projected = jnp.dot(sketches.astype(jnp.float32), basis_bf.astype(jnp.float32), preferred_element_type=jnp.float32)
    energy = lax.optimization_barrier(jnp.sum(projected * projected, axis=0))
    ordered = jnp.sort(energy)[::-1]
    threshold = lax.dynamic_index_in_dim(ordered, shrink_index[0], 0, keepdims=False)
    factor = jnp.sqrt(jnp.maximum(energy - threshold, 0.25 * threshold))
    return (basis * factor[None, :]).T
```

```python
import jax
import jax.numpy as jnp
from jax import lax
from jax.sharding import PartitionSpec as P

ITERS = 3
AXES = ("rows", "cols")
HIGHEST = lax.Precision.HIGHEST


def pieces(values):
    high = lax.reduce_precision(values, 8, 7)
    rest = values - high
    middle = lax.reduce_precision(rest, 8, 7)
    low = rest - middle
    return [part.astype(jnp.bfloat16) for part in (high, middle, low)]


def apply_sketches(strip, images):
    stacked = jnp.concatenate(pieces(images), axis=1)
    products = jnp.dot(strip, stacked, preferred_element_type=jnp.float32)
    high, middle, low = jnp.split(products, 3, axis=1)
    return high + (middle + low)


def all_sum(values):
    return lax.psum(values, AXES)


def inverse_factor(gram_total):
    lower_factor = jnp.linalg.cholesky(gram_total)
    identity = jnp.eye(gram_total.shape[0], dtype=jnp.float32)
    return jax.scipy.linalg.solve_triangular(lower_factor, identity, lower=True)


def body(sketches, start_basis, shrink_index):
    size = lax.axis_size("rows")
    strip = lax.all_to_all(sketches, "rows", split_axis=1, concat_axis=0, tiled=True)
    width = start_basis.shape[0] // size
    own_basis = lax.dynamic_slice_in_dim(start_basis, lax.axis_index("rows") * width, width, 0)
    projected = all_sum(jnp.dot(strip, own_basis, preferred_element_type=jnp.float32))
    for loop_index in range(ITERS):
        projected_bf = projected.astype(jnp.bfloat16)
        images = jnp.einsum("lw,lk->wk", strip, projected_bf, preferred_element_type=jnp.float32)
        raw = all_sum(apply_sketches(strip, images))
        gram_total = jnp.dot(projected_bf.astype(jnp.float32).T, raw, precision=HIGHEST)
        gram_total = 0.5 * (gram_total + gram_total.T)
        inverse = inverse_factor(gram_total)
        projected = jnp.dot(raw, inverse.T, precision=HIGHEST)
    energy = jnp.sum(projected * projected, axis=0)
    ordered = jnp.sort(energy)[::-1]
    threshold = lax.dynamic_index_in_dim(ordered, shrink_index[0], 0, keepdims=False)
    factor = jnp.sqrt(jnp.maximum(energy - threshold, 0.25 * threshold))
    scaled = jnp.dot(inverse * factor[:, None], images.T, precision=HIGHEST)
    return lax.all_to_all(scaled, "rows", split_axis=0, concat_axis=1, tiled=True)


def solution(mesh):
    return jax.shard_map(
        body,
        mesh=mesh,
        in_specs=(P("rows", "cols"), P("cols", None), P()),
        out_specs=P("rows", "cols"),
        check_vma=False,
    )
```

```python
import functools

import jax
import jax.numpy as jnp
from jax import lax
from jax.experimental import pallas as pl
from jax.experimental.pallas import tpu as pltpu
from jax.sharding import PartitionSpec as P

ITERS = 3
AXES = ("rows", "cols")
HIGHEST = lax.Precision.HIGHEST


def pieces(values):
    high = lax.reduce_precision(values, 8, 7)
    rest = values - high
    middle = lax.reduce_precision(rest, 8, 7)
    low = rest - middle
    return [part.astype(jnp.bfloat16) for part in (high, middle, low)]


def apply_sketches(strip, images):
    stacked = jnp.concatenate(pieces(images), axis=1)
    products = jnp.dot(strip, stacked, preferred_element_type=jnp.float32)
    high, middle, low = jnp.split(products, 3, axis=1)
    return high + (middle + low)


def path_orders(sizes):
    cols_bits = [("cols", 1 << bit) for bit in range(sizes["cols"].bit_length() - 1)]
    rows_bits = [("rows", 1 << bit) for bit in range(sizes["rows"].bit_length() - 1)]
    first = cols_bits + rows_bits
    second = cols_bits[:1] + rows_bits[:1] + cols_bits[1:] + rows_bits[1:]
    return [first, second]


def sum_kernel(orders, x_ref, out_ref, partial, arrived, send_sems, recv_sems):
    index = {axis: lax.axis_index(axis) for axis in AXES}
    stages = len(orders[0])
    rows = x_ref.shape[0] // len(orders)

    def side_of(axis, step):
        return lax.rem(index[axis] // step, 2)

    def partner_of(axis, step):
        return {axis: index[axis] + step * (1 - 2 * side_of(axis, step))}

    barrier = pltpu.get_barrier_semaphore()
    for axis, step in orders[0]:
        pl.semaphore_signal(
            barrier, inc=1, device_id=partner_of(axis, step), device_id_type=pl.DeviceIdType.MESH
        )
    pl.semaphore_wait(barrier, stages)

    copies = []

    def send(path, phase, stage, src, dst):
        copy = pltpu.make_async_remote_copy(
            src_ref=src,
            dst_ref=dst,
            send_sem=send_sems.at[path, phase, stage],
            recv_sem=recv_sems.at[path, phase, stage],
            device_id=partner_of(*orders[path][stage]),
            device_id_type=pl.DeviceIdType.MESH,
        )
        copy.start()
        copies.append(copy)
        return copy

    def span(start, size):
        return pl.ds(pl.multiple_of(start, 8), size)

    lows = [path * rows for path in range(len(orders))]
    trail = [[] for _ in orders]
    pending = [None for _ in orders]

    def halve(path, stage):
        half = rows >> (stage + 1)
        side = side_of(*orders[path][stage])
        source = x_ref if stage == 0 else partial
        slot = path * rows + rows - (rows >> stage)
        pending[path] = send(
            path, 0, stage,
            source.at[span(lows[path] + (1 - side) * half, half), :],
            arrived.at[slot : slot + half, :],
        )
        trail[path].append(lows[path])
        lows[path] = lows[path] + side * half

    for path in range(len(orders)):
        halve(path, 0)
    for stage in range(stages):
        half = rows >> (stage + 1)
        for path in range(len(orders)):
            pending[path].wait_recv()
            slot = path * rows + rows - (rows >> stage)
            own = span(lows[path], half)
            source = x_ref if stage == 0 else partial
            target = out_ref if stage == stages - 1 else partial
            target[own, :] = source[own, :] + arrived[slot : slot + half, :]
            if stage + 1 < stages:
                halve(path, stage + 1)
            else:
                own_rows = out_ref.at[own, :]
                pending[path] = send(path, 1, stage, own_rows, own_rows)
    for stage in reversed(range(stages)):
        for path in range(len(orders)):
            pending[path].wait_recv()
            if stage > 0:
                held = out_ref.at[span(trail[path][stage], rows >> stage), :]
                pending[path] = send(path, 1, stage - 1, held, held)
    for copy in copies:
        copy.wait_send()


def all_sum(values):
    sizes = {axis: lax.axis_size(axis) for axis in AXES}
    orders = path_orders(sizes)
    stages = len(orders[0])
    return pl.pallas_call(
        functools.partial(sum_kernel, orders),
        out_shape=jax.ShapeDtypeStruct(values.shape, jnp.float32),
        in_specs=[pl.BlockSpec(memory_space=pltpu.VMEM)],
        out_specs=pl.BlockSpec(memory_space=pltpu.VMEM),
        scratch_shapes=[
            pltpu.VMEM(values.shape, jnp.float32),
            pltpu.VMEM(values.shape, jnp.float32),
            pltpu.SemaphoreType.DMA((len(orders), 2, stages)),
            pltpu.SemaphoreType.DMA((len(orders), 2, stages)),
        ],
        compiler_params=pltpu.CompilerParams(
            collective_id=0, has_side_effects=True, vmem_limit_bytes=48 << 20
        ),
        name="all_sum",
    )(values)


def inverse_factor(gram_total):
    lower_factor = jnp.linalg.cholesky(gram_total)
    identity = jnp.eye(gram_total.shape[0], dtype=jnp.float32)
    return jax.scipy.linalg.solve_triangular(lower_factor, identity, lower=True)


def body(sketches, start_basis, shrink_index):
    size = lax.axis_size("rows")
    strip = lax.all_to_all(sketches, "rows", split_axis=1, concat_axis=0, tiled=True)
    width = start_basis.shape[0] // size
    own_basis = lax.dynamic_slice_in_dim(start_basis, lax.axis_index("rows") * width, width, 0)
    projected = all_sum(jnp.dot(strip, own_basis, preferred_element_type=jnp.float32))
    for loop_index in range(ITERS):
        projected_bf = projected.astype(jnp.bfloat16)
        images = jnp.einsum("lw,lk->wk", strip, projected_bf, preferred_element_type=jnp.float32)
        raw = all_sum(apply_sketches(strip, images))
        gram_total = jnp.dot(projected_bf.astype(jnp.float32).T, raw, precision=HIGHEST)
        gram_total = 0.5 * (gram_total + gram_total.T)
        inverse = inverse_factor(gram_total)
        projected = jnp.dot(raw, inverse.T, precision=HIGHEST)
    energy = jnp.sum(projected * projected, axis=0)
    ordered = jnp.sort(energy)[::-1]
    threshold = lax.dynamic_index_in_dim(ordered, shrink_index[0], 0, keepdims=False)
    factor = jnp.sqrt(jnp.maximum(energy - threshold, 0.25 * threshold))
    scaled = jnp.dot(inverse * factor[:, None], images.T, precision=HIGHEST)
    return lax.all_to_all(scaled, "rows", split_axis=0, concat_axis=1, tiled=True)


def solution(mesh):
    return jax.shard_map(
        body,
        mesh=mesh,
        in_specs=(P("rows", "cols"), P("cols", None), P()),
        out_specs=P("rows", "cols"),
        check_vma=False,
    )
```

```python
import functools

import jax
import jax.numpy as jnp
from jax import lax
from jax.experimental import pallas as pl
from jax.experimental.pallas import tpu as pltpu
from jax.sharding import PartitionSpec as P

ITERS = 3
AXES = ("rows", "cols")
HIGHEST = lax.Precision.HIGHEST


def pieces(values):
    high = lax.reduce_precision(values, 8, 7)
    rest = values - high
    middle = lax.reduce_precision(rest, 8, 7)
    low = rest - middle
    return [part.astype(jnp.bfloat16) for part in (high, middle, low)]


def apply_sketches(strip, images):
    stacked = jnp.concatenate(pieces(images), axis=1)
    products = jnp.dot(strip, stacked, preferred_element_type=jnp.float32)
    high, middle, low = jnp.split(products, 3, axis=1)
    return high + (middle + low)


def path_orders(sizes):
    cols_bits = [("cols", 1 << bit) for bit in range(sizes["cols"].bit_length() - 1)]
    rows_bits = [("rows", 1 << bit) for bit in range(sizes["rows"].bit_length() - 1)]
    first = cols_bits + rows_bits
    second = cols_bits[:1] + rows_bits[:1] + cols_bits[1:] + rows_bits[1:]
    return [first, second]


def sum_kernel(orders, x_ref, out_ref, partial, arrived, send_sems, recv_sems):
    index = {axis: lax.axis_index(axis) for axis in AXES}
    stages = len(orders[0])
    rows = x_ref.shape[0] // len(orders)

    def side_of(axis, step):
        return lax.rem(index[axis] // step, 2)

    def partner_of(axis, step):
        return {axis: index[axis] + step * (1 - 2 * side_of(axis, step))}

    barrier = pltpu.get_barrier_semaphore()
    for axis, step in orders[0]:
        pl.semaphore_signal(
            barrier, inc=1, device_id=partner_of(axis, step), device_id_type=pl.DeviceIdType.MESH
        )
    pl.semaphore_wait(barrier, stages)

    copies = []

    def send(path, phase, stage, src, dst):
        copy = pltpu.make_async_remote_copy(
            src_ref=src,
            dst_ref=dst,
            send_sem=send_sems.at[path, phase, stage],
            recv_sem=recv_sems.at[path, phase, stage],
            device_id=partner_of(*orders[path][stage]),
            device_id_type=pl.DeviceIdType.MESH,
        )
        copy.start()
        copies.append(copy)
        return copy

    def span(start, size):
        return pl.ds(pl.multiple_of(start, 8), size)

    lows = [path * rows for path in range(len(orders))]
    trail = [[] for _ in orders]
    pending = [None for _ in orders]

    def halve(path, stage):
        half = rows >> (stage + 1)
        side = side_of(*orders[path][stage])
        source = x_ref if stage == 0 else partial
        slot = path * rows + rows - (rows >> stage)
        pending[path] = send(
            path, 0, stage,
            source.at[span(lows[path] + (1 - side) * half, half), :],
            arrived.at[slot : slot + half, :],
        )
        trail[path].append(lows[path])
        lows[path] = lows[path] + side * half

    for path in range(len(orders)):
        halve(path, 0)
    for stage in range(stages):
        half = rows >> (stage + 1)
        for path in range(len(orders)):
            pending[path].wait_recv()
            slot = path * rows + rows - (rows >> stage)
            own = span(lows[path], half)
            source = x_ref if stage == 0 else partial
            target = out_ref if stage == stages - 1 else partial
            target[own, :] = source[own, :] + arrived[slot : slot + half, :]
            if stage + 1 < stages:
                halve(path, stage + 1)
            else:
                own_rows = out_ref.at[own, :]
                pending[path] = send(path, 1, stage, own_rows, own_rows)
    for stage in reversed(range(stages)):
        for path in range(len(orders)):
            pending[path].wait_recv()
            if stage > 0:
                held = out_ref.at[span(trail[path][stage], rows >> stage), :]
                pending[path] = send(path, 1, stage - 1, held, held)
    for copy in copies:
        copy.wait_send()


def all_sum(values):
    sizes = {axis: lax.axis_size(axis) for axis in AXES}
    orders = path_orders(sizes)
    stages = len(orders[0])
    return pl.pallas_call(
        functools.partial(sum_kernel, orders),
        out_shape=jax.ShapeDtypeStruct(values.shape, jnp.float32),
        in_specs=[pl.BlockSpec(memory_space=pltpu.VMEM)],
        out_specs=pl.BlockSpec(memory_space=pltpu.VMEM),
        scratch_shapes=[
            pltpu.VMEM(values.shape, jnp.float32),
            pltpu.VMEM(values.shape, jnp.float32),
            pltpu.SemaphoreType.DMA((len(orders), 2, stages)),
            pltpu.SemaphoreType.DMA((len(orders), 2, stages)),
        ],
        compiler_params=pltpu.CompilerParams(
            collective_id=0, has_side_effects=True, vmem_limit_bytes=48 << 20
        ),
        name="all_sum",
    )(values)


TILE = 128
SUBLANES = 8


def dot_full(left, right, contract=((1,), (0,))):
    return lax.dot_general(
        left, right, (contract, ((), ())), precision=HIGHEST, preferred_element_type=jnp.float32
    )


def eliminate(block):
    count = TILE // SUBLANES
    row_at = lax.broadcasted_iota(jnp.int32, (SUBLANES, TILE), 0)
    lane_at = lax.broadcasted_iota(jnp.int32, (SUBLANES, TILE), 1)
    left = [block[v * SUBLANES : (v + 1) * SUBLANES, :] for v in range(count)]
    right = [(lane_at == row_at + v * SUBLANES).astype(jnp.float32) for v in range(count)]
    done = []
    pivots = jnp.ones((SUBLANES, TILE), jnp.float32)
    for j in range(TILE):
        first, k = divmod(j, SUBLANES)
        column = jnp.broadcast_to(left[first][:, j : j + 1], (SUBLANES, TILE))
        pivot = column[k : k + 1, :]
        inverse = 1.0 / pivot
        left_row = left[first][k : k + 1, :] * inverse
        right_row = right[first][k : k + 1, :] * inverse
        pivots = jnp.where(row_at == k, jnp.broadcast_to(pivot, (SUBLANES, TILE)), pivots)
        for v in range(first, count):
            if v == first:
                scale = jnp.where(row_at > k, column, 0.0)
            else:
                scale = jnp.broadcast_to(left[v][:, j : j + 1], (SUBLANES, TILE))
            left[v] = left[v] - scale * left_row
            right[v] = right[v] - scale * right_row
        if k == SUBLANES - 1:
            done.append(right[first] / jnp.sqrt(pivots))
    return jnp.concatenate(done, axis=0)


def factor_kernel(gram_ref, inverse_ref):
    size = gram_ref.shape[0]
    inverse_ref[...] = jnp.zeros_like(inverse_ref)
    for start in range(0, size, TILE):
        here = slice(start, start + TILE)
        block = gram_ref[here, here]
        if start > 0:
            known = inverse_ref[:start, :start]
            lower = dot_full(gram_ref[here, :start], known, ((1,), (1,)))
            block = block - dot_full(lower, lower, ((1,), (1,)))
        own = eliminate(block)
        inverse_ref[here, here] = own
        if start > 0:
            inverse_ref[here, :start] = -dot_full(own, dot_full(lower, known))


def inverse_factor(gram_total):
    return pl.pallas_call(
        factor_kernel,
        out_shape=jax.ShapeDtypeStruct(gram_total.shape, jnp.float32),
        in_specs=[pl.BlockSpec(memory_space=pltpu.VMEM)],
        out_specs=pl.BlockSpec(memory_space=pltpu.VMEM),
        name="factor",
    )(gram_total)


def body(sketches, start_basis, shrink_index):
    size = lax.axis_size("rows")
    strip = lax.all_to_all(sketches, "rows", split_axis=1, concat_axis=0, tiled=True)
    width = start_basis.shape[0] // size
    own_basis = lax.dynamic_slice_in_dim(start_basis, lax.axis_index("rows") * width, width, 0)
    projected = all_sum(jnp.dot(strip, own_basis, preferred_element_type=jnp.float32))
    for loop_index in range(ITERS):
        projected_bf = projected.astype(jnp.bfloat16)
        images = jnp.einsum("lw,lk->wk", strip, projected_bf, preferred_element_type=jnp.float32)
        raw = all_sum(apply_sketches(strip, images))
        gram_total = jnp.dot(projected_bf.astype(jnp.float32).T, raw, precision=HIGHEST)
        gram_total = 0.5 * (gram_total + gram_total.T)
        inverse = inverse_factor(gram_total)
        projected = jnp.dot(raw, inverse.T, precision=HIGHEST)
    energy = jnp.sum(projected * projected, axis=0)
    ordered = jnp.sort(energy)[::-1]
    threshold = lax.dynamic_index_in_dim(ordered, shrink_index[0], 0, keepdims=False)
    factor = jnp.sqrt(jnp.maximum(energy - threshold, 0.25 * threshold))
    scaled = jnp.dot(inverse * factor[:, None], images.T, precision=HIGHEST)
    return lax.all_to_all(scaled, "rows", split_axis=0, concat_axis=1, tiled=True)


def solution(mesh):
    return jax.shard_map(
        body,
        mesh=mesh,
        in_specs=(P("rows", "cols"), P("cols", None), P()),
        out_specs=P("rows", "cols"),
        check_vma=False,
    )
```

```python
import functools

import jax
import jax.numpy as jnp
from jax import lax
from jax.experimental import pallas as pl
from jax.experimental.pallas import tpu as pltpu
from jax.sharding import PartitionSpec as P

ITERS = 3
AXES = ("rows", "cols")
HIGHEST = lax.Precision.HIGHEST


def pieces(values):
    high = lax.reduce_precision(values, 8, 7)
    rest = values - high
    middle = lax.reduce_precision(rest, 8, 7)
    low = rest - middle
    return [part.astype(jnp.bfloat16) for part in (high, middle, low)]


def apply_sketches(strip, images):
    stacked = jnp.concatenate(pieces(images), axis=1)
    products = jnp.dot(strip, stacked, preferred_element_type=jnp.float32)
    high, middle, low = jnp.split(products, 3, axis=1)
    return high + (middle + low)


def path_orders(sizes):
    cols_bits = [("cols", 1 << bit) for bit in range(sizes["cols"].bit_length() - 1)]
    rows_bits = [("rows", 1 << bit) for bit in range(sizes["rows"].bit_length() - 1)]
    first = cols_bits + rows_bits
    second = cols_bits[:1] + rows_bits[:1] + cols_bits[1:] + rows_bits[1:]
    return [first, second]


def sum_kernel(orders, x_ref, out_ref, partial, arrived, send_sems, recv_sems):
    index = {axis: lax.axis_index(axis) for axis in AXES}
    stages = len(orders[0])
    rows = x_ref.shape[0] // len(orders)

    def side_of(axis, step):
        return lax.rem(index[axis] // step, 2)

    def partner_of(axis, step):
        return {axis: index[axis] + step * (1 - 2 * side_of(axis, step))}

    barrier = pltpu.get_barrier_semaphore()
    for axis, step in orders[0]:
        pl.semaphore_signal(
            barrier, inc=1, device_id=partner_of(axis, step), device_id_type=pl.DeviceIdType.MESH
        )
    pl.semaphore_wait(barrier, stages)

    copies = []

    def send(path, phase, stage, src, dst):
        copy = pltpu.make_async_remote_copy(
            src_ref=src,
            dst_ref=dst,
            send_sem=send_sems.at[path, phase, stage],
            recv_sem=recv_sems.at[path, phase, stage],
            device_id=partner_of(*orders[path][stage]),
            device_id_type=pl.DeviceIdType.MESH,
        )
        copy.start()
        copies.append(copy)
        return copy

    def span(start, size):
        return pl.ds(pl.multiple_of(start, 8), size)

    lows = [path * rows for path in range(len(orders))]
    trail = [[] for _ in orders]
    pending = [None for _ in orders]

    def halve(path, stage):
        half = rows >> (stage + 1)
        side = side_of(*orders[path][stage])
        source = x_ref if stage == 0 else partial
        slot = path * rows + rows - (rows >> stage)
        pending[path] = send(
            path, 0, stage,
            source.at[span(lows[path] + (1 - side) * half, half), :],
            arrived.at[slot : slot + half, :],
        )
        trail[path].append(lows[path])
        lows[path] = lows[path] + side * half

    for path in range(len(orders)):
        halve(path, 0)
    for stage in range(stages):
        half = rows >> (stage + 1)
        for path in range(len(orders)):
            pending[path].wait_recv()
            slot = path * rows + rows - (rows >> stage)
            own = span(lows[path], half)
            source = x_ref if stage == 0 else partial
            target = out_ref if stage == stages - 1 else partial
            target[own, :] = source[own, :] + arrived[slot : slot + half, :]
            if stage + 1 < stages:
                halve(path, stage + 1)
            else:
                own_rows = out_ref.at[own, :]
                pending[path] = send(path, 1, stage, own_rows, own_rows)
    for stage in reversed(range(stages)):
        for path in range(len(orders)):
            pending[path].wait_recv()
            if stage > 0:
                held = out_ref.at[span(trail[path][stage], rows >> stage), :]
                pending[path] = send(path, 1, stage - 1, held, held)
    for copy in copies:
        copy.wait_send()


def all_sum(values):
    sizes = {axis: lax.axis_size(axis) for axis in AXES}
    orders = path_orders(sizes)
    stages = len(orders[0])
    return pl.pallas_call(
        functools.partial(sum_kernel, orders),
        out_shape=jax.ShapeDtypeStruct(values.shape, jnp.float32),
        in_specs=[pl.BlockSpec(memory_space=pltpu.VMEM)],
        out_specs=pl.BlockSpec(memory_space=pltpu.VMEM),
        scratch_shapes=[
            pltpu.VMEM(values.shape, jnp.float32),
            pltpu.VMEM(values.shape, jnp.float32),
            pltpu.SemaphoreType.DMA((len(orders), 2, stages)),
            pltpu.SemaphoreType.DMA((len(orders), 2, stages)),
        ],
        compiler_params=pltpu.CompilerParams(
            collective_id=0, has_side_effects=True, vmem_limit_bytes=48 << 20
        ),
        name="all_sum",
    )(values)


def start_kernel(sizes, x_ref, out_ref, partial, arrived, send_sems, recv_sems):
    index = {axis: lax.axis_index(axis) for axis in AXES}
    bits = {axis: [1 << bit for bit in range(sizes[axis].bit_length() - 1)] for axis in AXES}

    def side_of(axis, step):
        return lax.rem(index[axis] // step, 2)

    def partner_of(axis, step):
        return {axis: index[axis] + step * (1 - 2 * side_of(axis, step))}

    barrier = pltpu.get_barrier_semaphore()
    for axis in AXES:
        for step in bits[axis]:
            pl.semaphore_signal(
                barrier, inc=1, device_id=partner_of(axis, step), device_id_type=pl.DeviceIdType.MESH
            )
    pl.semaphore_wait(barrier, len(bits["rows"]) + len(bits["cols"]))

    copies = []

    def send(axis, step, src, dst):
        number = len(copies)
        copy = pltpu.make_async_remote_copy(
            src_ref=src,
            dst_ref=dst,
            send_sem=send_sems.at[number],
            recv_sem=recv_sems.at[number],
            device_id=partner_of(axis, step),
            device_id_type=pl.DeviceIdType.MESH,
        )
        copy.start()
        copies.append(copy)
        copy.wait_recv()

    def span(start, size):
        return pl.ds(pl.multiple_of(start, 16), size)

    count = x_ref.shape[0]
    low = 0
    lows = []
    source = x_ref
    for step in bits["cols"]:
        half = count // 2
        side = side_of("cols", step)
        slot = x_ref.shape[0] - count
        send(
            "cols", step,
            source.at[span(low + (1 - side) * half, half), :],
            arrived.at[slot : slot + half, :],
        )
        lows.append(low)
        low = low + side * half
        own = span(low, half)
        partial[own, :] = source[own, :] + arrived[slot : slot + half, :]
        source = partial
        count = half
    me = index["rows"]
    out_ref[pl.ds(me, 1), span(low, count), :] = source[span(low, count), :].astype(out_ref.dtype)[None]
    for step in bits["rows"]:
        held = out_ref.at[pl.ds(me // step * step, step), span(low, count), :]
        send("rows", step, held, held)
    for step, before in zip(reversed(bits["cols"]), reversed(lows)):
        held = out_ref.at[:, span(low, count), :]
        send("cols", step, held, held)
        low = before
        count = count * 2
    for copy in copies:
        copy.wait_send()


def start_sum(values):
    sizes = {axis: lax.axis_size(axis) for axis in AXES}
    sends = 2 * (sizes["cols"].bit_length() - 1) + sizes["rows"].bit_length() - 1
    owned, rank = values.shape
    gathered = pl.pallas_call(
        functools.partial(start_kernel, sizes),
        out_shape=jax.ShapeDtypeStruct((sizes["rows"], owned, rank), jnp.bfloat16),
        in_specs=[pl.BlockSpec(memory_space=pltpu.VMEM)],
        out_specs=pl.BlockSpec(memory_space=pltpu.VMEM),
        scratch_shapes=[
            pltpu.VMEM(values.shape, jnp.float32),
            pltpu.VMEM(values.shape, jnp.float32),
            pltpu.SemaphoreType.DMA((sends,)),
            pltpu.SemaphoreType.DMA((sends,)),
        ],
        compiler_params=pltpu.CompilerParams(
            collective_id=1, has_side_effects=True, vmem_limit_bytes=32 << 20
        ),
        name="start_sum",
    )(values)
    return gathered.reshape(sizes["rows"] * owned, rank)


TILE = 128
SUBLANES = 8


def dot_full(left, right, contract=((1,), (0,))):
    return lax.dot_general(
        left, right, (contract, ((), ())), precision=HIGHEST, preferred_element_type=jnp.float32
    )


def eliminate(block):
    count = TILE // SUBLANES
    row_at = lax.broadcasted_iota(jnp.int32, (SUBLANES, TILE), 0)
    lane_at = lax.broadcasted_iota(jnp.int32, (SUBLANES, TILE), 1)
    left = [block[v * SUBLANES : (v + 1) * SUBLANES, :] for v in range(count)]
    right = [(lane_at == row_at + v * SUBLANES).astype(jnp.float32) for v in range(count)]
    done = []
    pivots = jnp.ones((SUBLANES, TILE), jnp.float32)
    def spread(row):
        return jnp.broadcast_to(row, (SUBLANES, TILE))

    for j in range(0, TILE, 2):
        first, k = divmod(j, SUBLANES)
        ahead = spread(left[first][:, j : j + 1])
        behind = spread(left[first][:, j + 1 : j + 2])
        pivot = ahead[k : k + 1, :]
        inverse = 1.0 / pivot
        down = ahead[k + 1 : k + 2, :] * inverse
        across = behind[k : k + 1, :] * inverse
        next_pivot = behind[k + 1 : k + 2, :] - down * behind[k : k + 1, :]
        next_inverse = 1.0 / next_pivot
        rows = []
        for side in (left, right):
            row = side[first][k : k + 1, :]
            next_row = side[first][k + 1 : k + 2, :] - down * row
            rows.append((row * inverse, next_row * next_inverse))
        pivots = jnp.where(row_at == k, spread(pivot), pivots)
        pivots = jnp.where(row_at == k + 1, spread(next_pivot), pivots)
        for v in range(first, count):
            if v == first:
                scale, next_scale = ahead, behind - ahead * across
                scale = jnp.where(row_at > k, scale, 0.0)
                next_scale = jnp.where(row_at > k + 1, next_scale, 0.0)
            else:
                scale = spread(left[v][:, j : j + 1])
                next_scale = spread(left[v][:, j + 1 : j + 2]) - scale * across
            left[v] = left[v] - scale * rows[0][0] - next_scale * rows[0][1]
            right[v] = right[v] - scale * rows[1][0] - next_scale * rows[1][1]
        if k == SUBLANES - 2:
            done.append(right[first] / jnp.sqrt(pivots))
    return jnp.concatenate(done, axis=0)


def factor_kernel(gram_ref, inverse_ref):
    size = gram_ref.shape[0]
    inverse_ref[...] = jnp.zeros_like(inverse_ref)
    for start in range(0, size, TILE):
        here = slice(start, start + TILE)
        block = gram_ref[here, here]
        if start > 0:
            known = inverse_ref[:start, :start]
            lower = dot_full(gram_ref[here, :start], known, ((1,), (1,)))
            block = block - dot_full(lower, lower, ((1,), (1,)))
        own = eliminate(block)
        inverse_ref[here, here] = own
        if start > 0:
            inverse_ref[here, :start] = -dot_full(own, dot_full(lower, known))


def inverse_factor(gram_total):
    return pl.pallas_call(
        factor_kernel,
        out_shape=jax.ShapeDtypeStruct(gram_total.shape, jnp.float32),
        in_specs=[pl.BlockSpec(memory_space=pltpu.VMEM)],
        out_specs=pl.BlockSpec(memory_space=pltpu.VMEM),
        name="factor",
    )(gram_total)


def body(sketches, start_basis, shrink_index):
    strip = lax.all_to_all(sketches, "rows", split_axis=1, concat_axis=0, tiled=True)
    projected_bf = start_sum(jnp.dot(sketches, start_basis, preferred_element_type=jnp.float32))
    for loop_index in range(ITERS):
        if loop_index > 0:
            projected_bf = projected.astype(jnp.bfloat16)
        images = jnp.einsum("lw,lk->wk", strip, projected_bf, preferred_element_type=jnp.float32)
        raw = all_sum(apply_sketches(strip, images))
        gram_total = jnp.dot(projected_bf.astype(jnp.float32).T, raw, precision=HIGHEST)
        gram_total = 0.5 * (gram_total + gram_total.T)
        inverse = inverse_factor(gram_total)
        projected = jnp.dot(raw, inverse.T, precision=HIGHEST)
    energy = jnp.sum(projected * projected, axis=0)
    ordered = jnp.sort(energy)[::-1]
    threshold = lax.dynamic_index_in_dim(ordered, shrink_index[0], 0, keepdims=False)
    factor = jnp.sqrt(jnp.maximum(energy - threshold, 0.25 * threshold))
    scaled = jnp.dot(inverse * factor[:, None], images.T, precision=HIGHEST)
    return lax.all_to_all(scaled, "rows", split_axis=0, concat_axis=1, tiled=True)


def solution(mesh):
    return jax.shard_map(
        body,
        mesh=mesh,
        in_specs=(P("rows", "cols"), P("cols", None), P()),
        out_specs=P("rows", "cols"),
        check_vma=False,
    )
```

```python
import functools

import jax
import jax.numpy as jnp
from jax import lax
from jax.experimental import pallas as pl
from jax.experimental.pallas import tpu as pltpu
from jax.sharding import PartitionSpec as P

ITERS = 3
AXES = ("rows", "cols")
HIGHEST = lax.Precision.HIGHEST


def pieces(values):
    high = lax.reduce_precision(values, 8, 7)
    rest = values - high
    middle = lax.reduce_precision(rest, 8, 7)
    low = rest - middle
    return [part.astype(jnp.bfloat16) for part in (high, middle, low)]


def apply_sketches(strip, images):
    stacked = jnp.concatenate(pieces(images), axis=1)
    products = jnp.dot(strip, stacked, preferred_element_type=jnp.float32)
    high, middle, low = jnp.split(products, 3, axis=1)
    return high + (middle + low)


def path_orders(sizes):
    cols_bits = [("cols", 1 << bit) for bit in range(sizes["cols"].bit_length() - 1)]
    rows_bits = [("rows", 1 << bit) for bit in range(sizes["rows"].bit_length() - 1)]
    first = cols_bits + rows_bits
    second = cols_bits[:1] + rows_bits + cols_bits[1:]
    return [first, second]


def sum_kernel(orders, x_ref, out_ref, partial, arrived, send_sems, recv_sems):
    index = {axis: lax.axis_index(axis) for axis in AXES}
    stages = len(orders[0])
    rows = x_ref.shape[0] // len(orders)

    def side_of(axis, step):
        return lax.rem(index[axis] // step, 2)

    def partner_of(axis, step):
        return {axis: index[axis] + step * (1 - 2 * side_of(axis, step))}

    barrier = pltpu.get_barrier_semaphore()
    for axis, step in orders[0]:
        pl.semaphore_signal(
            barrier, inc=1, device_id=partner_of(axis, step), device_id_type=pl.DeviceIdType.MESH
        )
    pl.semaphore_wait(barrier, stages)

    copies = []

    def send(path, phase, stage, src, dst):
        copy = pltpu.make_async_remote_copy(
            src_ref=src,
            dst_ref=dst,
            send_sem=send_sems.at[path, phase, stage],
            recv_sem=recv_sems.at[path, phase, stage],
            device_id=partner_of(*orders[path][stage]),
            device_id_type=pl.DeviceIdType.MESH,
        )
        copy.start()
        copies.append(copy)
        return copy

    def span(start, size):
        return pl.ds(pl.multiple_of(start, 8), size)

    lows = [path * rows for path in range(len(orders))]
    trail = [[] for _ in orders]
    pending = [None for _ in orders]

    def halve(path, stage):
        half = rows >> (stage + 1)
        side = side_of(*orders[path][stage])
        source = x_ref if stage == 0 else partial
        slot = path * rows + rows - (rows >> stage)
        pending[path] = send(
            path, 0, stage,
            source.at[span(lows[path] + (1 - side) * half, half), :],
            arrived.at[slot : slot + half, :],
        )
        trail[path].append(lows[path])
        lows[path] = lows[path] + side * half

    for path in range(len(orders)):
        halve(path, 0)
    for stage in range(stages):
        half = rows >> (stage + 1)
        for path in range(len(orders)):
            pending[path].wait_recv()
            slot = path * rows + rows - (rows >> stage)
            own = span(lows[path], half)
            source = x_ref if stage == 0 else partial
            target = out_ref if stage == stages - 1 else partial
            target[own, :] = source[own, :] + arrived[slot : slot + half, :]
            if stage + 1 < stages:
                halve(path, stage + 1)
            else:
                own_rows = out_ref.at[own, :]
                pending[path] = send(path, 1, stage, own_rows, own_rows)
    for stage in reversed(range(stages)):
        for path in range(len(orders)):
            pending[path].wait_recv()
            if stage > 0:
                held = out_ref.at[span(trail[path][stage], rows >> stage), :]
                pending[path] = send(path, 1, stage - 1, held, held)
    for copy in copies:
        copy.wait_send()


def all_sum(values):
    sizes = {axis: lax.axis_size(axis) for axis in AXES}
    orders = path_orders(sizes)
    stages = len(orders[0])
    return pl.pallas_call(
        functools.partial(sum_kernel, orders),
        out_shape=jax.ShapeDtypeStruct(values.shape, jnp.float32),
        in_specs=[pl.BlockSpec(memory_space=pltpu.VMEM)],
        out_specs=pl.BlockSpec(memory_space=pltpu.VMEM),
        scratch_shapes=[
            pltpu.VMEM(values.shape, jnp.float32),
            pltpu.VMEM(values.shape, jnp.float32),
            pltpu.SemaphoreType.DMA((len(orders), 2, stages)),
            pltpu.SemaphoreType.DMA((len(orders), 2, stages)),
        ],
        compiler_params=pltpu.CompilerParams(
            collective_id=0, has_side_effects=True, vmem_limit_bytes=48 << 20
        ),
        name="all_sum",
    )(values)


def start_kernel(sizes, x_ref, out_ref, partial, arrived, send_sems, recv_sems):
    index = {axis: lax.axis_index(axis) for axis in AXES}
    bits = {axis: [1 << bit for bit in range(sizes[axis].bit_length() - 1)] for axis in AXES}

    def side_of(axis, step):
        return lax.rem(index[axis] // step, 2)

    def partner_of(axis, step):
        return {axis: index[axis] + step * (1 - 2 * side_of(axis, step))}

    barrier = pltpu.get_barrier_semaphore()
    for axis in AXES:
        for step in bits[axis]:
            pl.semaphore_signal(
                barrier, inc=1, device_id=partner_of(axis, step), device_id_type=pl.DeviceIdType.MESH
            )
    pl.semaphore_wait(barrier, len(bits["rows"]) + len(bits["cols"]))

    copies = []

    def send(axis, step, src, dst):
        number = len(copies)
        copy = pltpu.make_async_remote_copy(
            src_ref=src,
            dst_ref=dst,
            send_sem=send_sems.at[number],
            recv_sem=recv_sems.at[number],
            device_id=partner_of(axis, step),
            device_id_type=pl.DeviceIdType.MESH,
        )
        copy.start()
        copies.append(copy)
        copy.wait_recv()

    def span(start, size):
        return pl.ds(pl.multiple_of(start, 16), size)

    count = x_ref.shape[0]
    low = 0
    lows = []
    source = x_ref
    for step in bits["cols"]:
        half = count // 2
        side = side_of("cols", step)
        slot = x_ref.shape[0] - count
        send(
            "cols", step,
            source.at[span(low + (1 - side) * half, half), :],
            arrived.at[slot : slot + half, :],
        )
        lows.append(low)
        low = low + side * half
        own = span(low, half)
        partial[own, :] = source[own, :] + arrived[slot : slot + half, :]
        source = partial
        count = half
    me = index["rows"]
    out_ref[pl.ds(me, 1), span(low, count), :] = source[span(low, count), :].astype(out_ref.dtype)[None]
    for step in bits["rows"]:
        held = out_ref.at[pl.ds(me // step * step, step), span(low, count), :]
        send("rows", step, held, held)
    for step, before in zip(reversed(bits["cols"]), reversed(lows)):
        held = out_ref.at[:, span(low, count), :]
        send("cols", step, held, held)
        low = before
        count = count * 2
    for copy in copies:
        copy.wait_send()


def start_sum(values):
    sizes = {axis: lax.axis_size(axis) for axis in AXES}
    sends = 2 * (sizes["cols"].bit_length() - 1) + sizes["rows"].bit_length() - 1
    owned, rank = values.shape
    gathered = pl.pallas_call(
        functools.partial(start_kernel, sizes),
        out_shape=jax.ShapeDtypeStruct((sizes["rows"], owned, rank), jnp.bfloat16),
        in_specs=[pl.BlockSpec(memory_space=pltpu.VMEM)],
        out_specs=pl.BlockSpec(memory_space=pltpu.VMEM),
        scratch_shapes=[
            pltpu.VMEM(values.shape, jnp.float32),
            pltpu.VMEM(values.shape, jnp.float32),
            pltpu.SemaphoreType.DMA((sends,)),
            pltpu.SemaphoreType.DMA((sends,)),
        ],
        compiler_params=pltpu.CompilerParams(
            collective_id=1, has_side_effects=True, vmem_limit_bytes=32 << 20
        ),
        name="start_sum",
    )(values)
    return gathered.reshape(sizes["rows"] * owned, rank)


TILE = 128
SUBLANES = 8
PIVOTS = 4


def dot_full(left, right, contract=((1,), (0,))):
    return lax.dot_general(
        left, right, (contract, ((), ())), precision=HIGHEST, preferred_element_type=jnp.float32
    )


def eliminate(block):
    count = TILE // SUBLANES
    row_at = lax.broadcasted_iota(jnp.int32, (SUBLANES, TILE), 0)
    lane_at = lax.broadcasted_iota(jnp.int32, (SUBLANES, TILE), 1)
    left = [block[v * SUBLANES : (v + 1) * SUBLANES, :] for v in range(count)]
    right = [(lane_at == row_at + v * SUBLANES).astype(jnp.float32) for v in range(count)]
    done = []
    pivots = jnp.ones((SUBLANES, TILE), jnp.float32)
    def spread(row):
        return jnp.broadcast_to(row, (SUBLANES, TILE))

    for j in range(0, TILE, PIVOTS):
        first, k = divmod(j, SUBLANES)
        heads = [spread(left[first][:, j + i : j + i + 1]) for i in range(PIVOTS)]
        inverses, across = [], {}
        for i in range(PIVOTS):
            pivot = heads[i][k + i : k + i + 1, :]
            inverses.append(1.0 / pivot)
            pivots = jnp.where(row_at == k + i, spread(pivot), pivots)
            below = jnp.where(row_at > k + i, heads[i], 0.0)
            for n in range(i + 1, PIVOTS):
                across[i, n] = heads[n][k + i : k + i + 1, :] * inverses[i]
                heads[n] = heads[n] - below * across[i, n]
            heads[i] = below
        rows = []
        for side in (left, right):
            current, scaled = side[first], []
            for i in range(PIVOTS):
                scaled.append(current[k + i : k + i + 1, :] * inverses[i])
                current = current - heads[i] * scaled[i]
            side[first] = current
            rows.append(scaled)
        for v in range(first + 1, count):
            scales = [spread(left[v][:, j + i : j + i + 1]) for i in range(PIVOTS)]
            for i in range(PIVOTS):
                for n in range(i + 1, PIVOTS):
                    scales[n] = scales[n] - scales[i] * across[i, n]
                left[v] = left[v] - scales[i] * rows[0][i]
                right[v] = right[v] - scales[i] * rows[1][i]
        if k + PIVOTS == SUBLANES:
            done.append(right[first] / jnp.sqrt(pivots))
    return jnp.concatenate(done, axis=0)


def factor_kernel(gram_ref, inverse_ref, work_ref, lower_ref):
    size = gram_ref.shape[0]
    inverse_ref[...] = jnp.zeros_like(inverse_ref)
    work_ref[...] = gram_ref[:TILE, :TILE]

    @pl.loop(0, size // TILE)
    def _(at):
        own = eliminate(work_ref[...])
        work_ref[...] = own
        for number in range(size // TILE):
            start, stop = number * TILE, (number + 1) * TILE
            here = slice(start, stop)

            @pl.when(at == number)
            def _():
                inverse_ref[here, here] = work_ref[...]
                if start > 0:
                    off = dot_full(lower_ref[:, :start], inverse_ref[:start, :start])
                    inverse_ref[here, :start] = -dot_full(work_ref[...], off)
                if stop < size:
                    after = slice(stop, stop + TILE)
                    lower = dot_full(gram_ref[after, :stop], inverse_ref[:stop, :stop], ((1,), (1,)))
                    lower_ref[:, :stop] = lower
                    work_ref[...] = gram_ref[after, after] - dot_full(lower, lower, ((1,), (1,)))


def inverse_factor(gram_total):
    return pl.pallas_call(
        factor_kernel,
        out_shape=jax.ShapeDtypeStruct(gram_total.shape, jnp.float32),
        in_specs=[pl.BlockSpec(memory_space=pltpu.VMEM)],
        out_specs=pl.BlockSpec(memory_space=pltpu.VMEM),
        scratch_shapes=[
            pltpu.VMEM((TILE, TILE), jnp.float32),
            pltpu.VMEM((TILE, gram_total.shape[0]), jnp.float32),
        ],
        name="factor",
    )(gram_total)


def body(sketches, start_basis, shrink_index):
    strip = lax.all_to_all(sketches, "rows", split_axis=1, concat_axis=0, tiled=True)
    projected_bf = start_sum(jnp.dot(sketches, start_basis, preferred_element_type=jnp.float32))
    for loop_index in range(ITERS):
        if loop_index > 0:
            projected_bf = projected.astype(jnp.bfloat16)
        images = jnp.einsum("lw,lk->wk", strip, projected_bf, preferred_element_type=jnp.float32)
        raw = all_sum(apply_sketches(strip, images))
        gram_total = jnp.dot(projected_bf.astype(jnp.float32).T, raw, precision=HIGHEST)
        gram_total = 0.5 * (gram_total + gram_total.T)
        inverse = inverse_factor(gram_total)
        projected = jnp.dot(raw, inverse.T, precision=HIGHEST)
    energy = jnp.sum(projected * projected, axis=0)
    ordered = jnp.sort(energy)[::-1]
    threshold = lax.dynamic_index_in_dim(ordered, shrink_index[0], 0, keepdims=False)
    factor = jnp.sqrt(jnp.maximum(energy - threshold, 0.25 * threshold))
    scaled = jnp.dot(inverse * factor[:, None], images.T, precision=HIGHEST)
    return lax.all_to_all(scaled, "rows", split_axis=0, concat_axis=1, tiled=True)


def solution(mesh):
    return jax.shard_map(
        body,
        mesh=mesh,
        in_specs=(P("rows", "cols"), P("cols", None), P()),
        out_specs=P("rows", "cols"),
        check_vma=False,
    )
```

```python
import functools

import jax
import jax.numpy as jnp
from jax import lax
from jax.experimental import pallas as pl
from jax.experimental.pallas import tpu as pltpu
from jax.sharding import PartitionSpec as P

ITERS = 3
AXES = ("rows", "cols")
HIGHEST = lax.Precision.HIGHEST


def pieces(values):
    high = lax.reduce_precision(values, 8, 7)
    rest = values - high
    middle = lax.reduce_precision(rest, 8, 7)
    low = rest - middle
    return [part.astype(jnp.bfloat16) for part in (high, middle, low)]


def apply_sketches(strip, images):
    stacked = jnp.concatenate(pieces(images), axis=1)
    products = jnp.dot(strip, stacked, preferred_element_type=jnp.float32)
    high, middle, low = jnp.split(products, 3, axis=1)
    return high + (middle + low)


def path_orders(sizes):
    cols_bits = [("cols", 1 << bit) for bit in range(sizes["cols"].bit_length() - 1)]
    rows_bits = [("rows", 1 << bit) for bit in range(sizes["rows"].bit_length() - 1)]
    first = cols_bits + rows_bits
    second = cols_bits[:1] + rows_bits[:1] + cols_bits[1:] + rows_bits[1:]
    return [first, second] * 2


def sum_kernel(orders, x_ref, out_ref, partial, arrived, send_sems, recv_sems):
    index = {axis: lax.axis_index(axis) for axis in AXES}
    stages = len(orders[0])
    rows = x_ref.shape[0] // len(orders)

    def side_of(axis, step):
        return lax.rem(index[axis] // step, 2)

    def partner_of(axis, step):
        return {axis: index[axis] + step * (1 - 2 * side_of(axis, step))}

    barrier = pltpu.get_barrier_semaphore()
    for axis, step in orders[0]:
        pl.semaphore_signal(
            barrier, inc=1, device_id=partner_of(axis, step), device_id_type=pl.DeviceIdType.MESH
        )
    pl.semaphore_wait(barrier, stages)

    copies = []

    def send(path, phase, stage, src, dst):
        copy = pltpu.make_async_remote_copy(
            src_ref=src,
            dst_ref=dst,
            send_sem=send_sems.at[path, phase, stage],
            recv_sem=recv_sems.at[path, phase, stage],
            device_id=partner_of(*orders[path][stage]),
            device_id_type=pl.DeviceIdType.MESH,
        )
        copy.start()
        copies.append(copy)
        return copy

    def span(start, size):
        return pl.ds(pl.multiple_of(start, 8), size)

    lows = [path * rows for path in range(len(orders))]
    trail = [[] for _ in orders]
    pending = [None for _ in orders]

    def halve(path, stage):
        half = rows >> (stage + 1)
        side = side_of(*orders[path][stage])
        source = x_ref if stage == 0 else partial
        slot = path * rows + rows - (rows >> stage)
        pending[path] = send(
            path, 0, stage,
            source.at[span(lows[path] + (1 - side) * half, half), :],
            arrived.at[slot : slot + half, :],
        )
        trail[path].append(lows[path])
        lows[path] = lows[path] + side * half

    for path in range(len(orders)):
        halve(path, 0)
    for stage in range(stages):
        half = rows >> (stage + 1)
        for path in range(len(orders)):
            pending[path].wait_recv()
            slot = path * rows + rows - (rows >> stage)
            own = span(lows[path], half)
            source = x_ref if stage == 0 else partial
            target = out_ref if stage == stages - 1 else partial
            target[own, :] = source[own, :] + arrived[slot : slot + half, :]
            if stage + 1 < stages:
                halve(path, stage + 1)
            else:
                own_rows = out_ref.at[own, :]
                pending[path] = send(path, 1, stage, own_rows, own_rows)
    for stage in reversed(range(stages)):
        for path in range(len(orders)):
            pending[path].wait_recv()
            if stage > 0:
                held = out_ref.at[span(trail[path][stage], rows >> stage), :]
                pending[path] = send(path, 1, stage - 1, held, held)
    for copy in copies:
        copy.wait_send()


def all_sum(values):
    sizes = {axis: lax.axis_size(axis) for axis in AXES}
    orders = path_orders(sizes)
    stages = len(orders[0])
    return pl.pallas_call(
        functools.partial(sum_kernel, orders),
        out_shape=jax.ShapeDtypeStruct(values.shape, jnp.float32),
        in_specs=[pl.BlockSpec(memory_space=pltpu.VMEM)],
        out_specs=pl.BlockSpec(memory_space=pltpu.VMEM),
        scratch_shapes=[
            pltpu.VMEM(values.shape, jnp.float32),
            pltpu.VMEM(values.shape, jnp.float32),
            pltpu.SemaphoreType.DMA((len(orders), 2, stages)),
            pltpu.SemaphoreType.DMA((len(orders), 2, stages)),
        ],
        compiler_params=pltpu.CompilerParams(
            collective_id=0, has_side_effects=True, vmem_limit_bytes=48 << 20
        ),
        name="all_sum",
    )(values)


def start_kernel(sizes, x_ref, out_ref, partial, arrived, send_sems, recv_sems):
    index = {axis: lax.axis_index(axis) for axis in AXES}
    bits = {axis: [1 << bit for bit in range(sizes[axis].bit_length() - 1)] for axis in AXES}

    def side_of(axis, step):
        return lax.rem(index[axis] // step, 2)

    def partner_of(axis, step):
        return {axis: index[axis] + step * (1 - 2 * side_of(axis, step))}

    barrier = pltpu.get_barrier_semaphore()
    for axis in AXES:
        for step in bits[axis]:
            pl.semaphore_signal(
                barrier, inc=1, device_id=partner_of(axis, step), device_id_type=pl.DeviceIdType.MESH
            )
    pl.semaphore_wait(barrier, len(bits["rows"]) + len(bits["cols"]))

    copies = []

    def send(axis, step, src, dst):
        number = len(copies)
        copy = pltpu.make_async_remote_copy(
            src_ref=src,
            dst_ref=dst,
            send_sem=send_sems.at[number],
            recv_sem=recv_sems.at[number],
            device_id=partner_of(axis, step),
            device_id_type=pl.DeviceIdType.MESH,
        )
        copy.start()
        copies.append(copy)
        copy.wait_recv()

    def span(start, size):
        return pl.ds(pl.multiple_of(start, 16), size)

    count = x_ref.shape[0]
    low = 0
    lows = []
    source = x_ref
    for step in bits["cols"]:
        half = count // 2
        side = side_of("cols", step)
        slot = x_ref.shape[0] - count
        send(
            "cols", step,
            source.at[span(low + (1 - side) * half, half), :],
            arrived.at[slot : slot + half, :],
        )
        lows.append(low)
        low = low + side * half
        own = span(low, half)
        partial[own, :] = source[own, :] + arrived[slot : slot + half, :]
        source = partial
        count = half
    me = index["rows"]
    out_ref[pl.ds(me, 1), span(low, count), :] = source[span(low, count), :].astype(out_ref.dtype)[None]
    for step in bits["rows"]:
        held = out_ref.at[pl.ds(me // step * step, step), span(low, count), :]
        send("rows", step, held, held)
    for step, before in zip(reversed(bits["cols"]), reversed(lows)):
        held = out_ref.at[:, span(low, count), :]
        send("cols", step, held, held)
        low = before
        count = count * 2
    for copy in copies:
        copy.wait_send()


def start_sum(values):
    sizes = {axis: lax.axis_size(axis) for axis in AXES}
    sends = 2 * (sizes["cols"].bit_length() - 1) + sizes["rows"].bit_length() - 1
    owned, rank = values.shape
    gathered = pl.pallas_call(
        functools.partial(start_kernel, sizes),
        out_shape=jax.ShapeDtypeStruct((sizes["rows"], owned, rank), jnp.bfloat16),
        in_specs=[pl.BlockSpec(memory_space=pltpu.VMEM)],
        out_specs=pl.BlockSpec(memory_space=pltpu.VMEM),
        scratch_shapes=[
            pltpu.VMEM(values.shape, jnp.float32),
            pltpu.VMEM(values.shape, jnp.float32),
            pltpu.SemaphoreType.DMA((sends,)),
            pltpu.SemaphoreType.DMA((sends,)),
        ],
        compiler_params=pltpu.CompilerParams(
            collective_id=1, has_side_effects=True, vmem_limit_bytes=32 << 20
        ),
        name="start_sum",
    )(values)
    return gathered.reshape(sizes["rows"] * owned, rank)


TILE = 128
SUBLANES = 8
PIVOTS = 4


def dot_full(left, right, contract=((1,), (0,))):
    return lax.dot_general(
        left, right, (contract, ((), ())), precision=HIGHEST, preferred_element_type=jnp.float32
    )


def eliminate(block):
    count = TILE // SUBLANES
    row_at = lax.broadcasted_iota(jnp.int32, (SUBLANES, TILE), 0)
    lane_at = lax.broadcasted_iota(jnp.int32, (SUBLANES, TILE), 1)
    left = [block[v * SUBLANES : (v + 1) * SUBLANES, :] for v in range(count)]
    right = [(lane_at == row_at + v * SUBLANES).astype(jnp.float32) for v in range(count)]
    done = []
    pivots = jnp.ones((SUBLANES, TILE), jnp.float32)
    def spread(row):
        return jnp.broadcast_to(row, (SUBLANES, TILE))

    for j in range(0, TILE, PIVOTS):
        first, k = divmod(j, SUBLANES)
        heads = [spread(left[first][:, j + i : j + i + 1]) for i in range(PIVOTS)]
        inverses, across = [], {}
        for i in range(PIVOTS):
            pivot = heads[i][k + i : k + i + 1, :]
            inverses.append(1.0 / pivot)
            pivots = jnp.where(row_at == k + i, spread(pivot), pivots)
            below = jnp.where(row_at > k + i, heads[i], 0.0)
            for n in range(i + 1, PIVOTS):
                across[i, n] = heads[n][k + i : k + i + 1, :] * inverses[i]
                heads[n] = heads[n] - below * across[i, n]
            heads[i] = below
        rows = []
        for side in (left, right):
            current, scaled = side[first], []
            for i in range(PIVOTS):
                scaled.append(current[k + i : k + i + 1, :] * inverses[i])
                current = current - heads[i] * scaled[i]
            side[first] = current
            rows.append(scaled)
        for v in range(first + 1, count):
            scales = [spread(left[v][:, j + i : j + i + 1]) for i in range(PIVOTS)]
            for i in range(PIVOTS):
                for n in range(i + 1, PIVOTS):
                    scales[n] = scales[n] - scales[i] * across[i, n]
                left[v] = left[v] - scales[i] * rows[0][i]
                right[v] = right[v] - scales[i] * rows[1][i]
        if k + PIVOTS == SUBLANES:
            done.append(right[first] / jnp.sqrt(pivots))
    return jnp.concatenate(done, axis=0)


def factor_kernel(gram_ref, inverse_ref, work_ref, lower_ref):
    size = gram_ref.shape[0]
    inverse_ref[...] = jnp.zeros_like(inverse_ref)
    work_ref[...] = gram_ref[:TILE, :TILE]

    @pl.loop(0, size // TILE)
    def _(at):
        own = eliminate(work_ref[...])
        work_ref[...] = own
        for number in range(size // TILE):
            start, stop = number * TILE, (number + 1) * TILE
            here = slice(start, stop)

            @pl.when(at == number)
            def _():
                inverse_ref[here, here] = work_ref[...]
                if start > 0:
                    off = dot_full(lower_ref[:, :start], inverse_ref[:start, :start])
                    inverse_ref[here, :start] = -dot_full(work_ref[...], off)
                if stop < size:
                    after = slice(stop, stop + TILE)
                    lower = dot_full(gram_ref[after, :stop], inverse_ref[:stop, :stop], ((1,), (1,)))
                    lower_ref[:, :stop] = lower
                    work_ref[...] = gram_ref[after, after] - dot_full(lower, lower, ((1,), (1,)))


def inverse_factor(gram_total):
    return pl.pallas_call(
        factor_kernel,
        out_shape=jax.ShapeDtypeStruct(gram_total.shape, jnp.float32),
        in_specs=[pl.BlockSpec(memory_space=pltpu.VMEM)],
        out_specs=pl.BlockSpec(memory_space=pltpu.VMEM),
        scratch_shapes=[
            pltpu.VMEM((TILE, TILE), jnp.float32),
            pltpu.VMEM((TILE, gram_total.shape[0]), jnp.float32),
        ],
        name="factor",
    )(gram_total)


def body(sketches, start_basis, shrink_index):
    strip = lax.all_to_all(sketches, "rows", split_axis=1, concat_axis=0, tiled=True)
    projected_bf = start_sum(jnp.dot(sketches, start_basis, preferred_element_type=jnp.float32))
    for loop_index in range(ITERS):
        if loop_index > 0:
            projected_bf = projected.astype(jnp.bfloat16)
        images = jnp.einsum("lw,lk->wk", strip, projected_bf, preferred_element_type=jnp.float32)
        raw = all_sum(apply_sketches(strip, images))
        gram_total = jnp.dot(projected_bf.astype(jnp.float32).T, raw, precision=HIGHEST)
        gram_total = 0.5 * (gram_total + gram_total.T)
        inverse = inverse_factor(gram_total)
        projected = jnp.dot(raw, inverse.T, precision=HIGHEST)
    energy = jnp.sum(projected * projected, axis=0)
    ordered = jnp.sort(energy)[::-1]
    threshold = lax.dynamic_index_in_dim(ordered, shrink_index[0], 0, keepdims=False)
    factor = jnp.sqrt(jnp.maximum(energy - threshold, 0.25 * threshold))
    scaled = jnp.dot(inverse * factor[:, None], images.T, precision=HIGHEST)
    return lax.all_to_all(scaled, "rows", split_axis=0, concat_axis=1, tiled=True)


def solution(mesh):
    return jax.shard_map(
        body,
        mesh=mesh,
        in_specs=(P("rows", "cols"), P("cols", None), P()),
        out_specs=P("rows", "cols"),
        check_vma=False,
    )
```
